32 devices in a mesh: seq: 8 (over z, y), lane: 4 (over x, core).
Axes of the slice: x: 2, y: 2, z: 4, core: 2. Of those that a mesh axis runs over, the one named last changes fastest.
Arguments:
- tokens_in: bfloat16 [3072, 8192], P('seq', 'lane'), may hold values from -6 to 6
- gate_weight: bfloat16 [8192, 1024], P(None, 'lane'), may hold values from -0.0625 to 0.0625
- up_weight: bfloat16 [8192, 1024], P(None, 'lane'), may hold values from -0.0625 to 0.0625
- output_grad: bfloat16 [3072, 4096], P('seq', 'lane'), may hold values from -0.15234375 to 0.15234375
- input_basis: float32 [1024, 1024], P('seq'), may hold values from -0.1875 to 0.1875
- output_basis: float32 [4, 1024, 1024], P('lane', 'seq'), may hold values from -0.1875 to 0.1875
- shard_order: int32 [8], replicated, may hold values from 0 to 7, each once
Outputs:
- eigenvalues: float32 [4, 1024, 1024], P('lane', 'seq')
The draws below stay inside these ranges and needn't reach their ends.
All inputs are finite; a program needn't handle non-finite values.
Results may differ from the reference program's by a relative error of at most 0.0029.
Values may be sent and summed in bfloat16 or wider, within the bound.
A program may use at most 128 MiB of HBM per device.

```python
import jax
import jax.numpy as jnp
from jax import lax

D = 8192
TILE = 1024
TOK_DEV = 384
TILES = 4
SHARDS = 8
TOKENS = 3072
LENGTH = 1536


def shard_levels(key, shape, shards, low, high):
    def one(axis_at, shards_of):
        steps = jax.random.uniform(jax.random.fold_in(jax.random.fold_in(key, 6), axis_at), (shards_of,), jnp.float32, low / len(shards), high / len(shards))
        return jnp.repeat(jnp.exp(steps), shape[axis_at] // shards_of).reshape((-1,) + (1,) * (len(shape) - axis_at - 1))

    level = one(*shards[0])
    for cut in shards[1:]:
        level = level * one(*cut)
    return level


def centred(stream_key, shape, spread, bound, shards=(), kind=jnp.bfloat16):
    drawn = spread * jax.random.normal(stream_key, shape, jnp.float32)
    if shards:
        drawn = drawn * shard_levels(stream_key, shape, shards, -0.22, 0.18)
    return jnp.clip(drawn, -bound, bound).astype(kind)


def setup_inputs(seed: int = 0) -> dict:
    seeds = jax.random.split(jax.random.key(seed), 8)
    tokens_in = centred(seeds[0], (TOKENS, D), 1.0, 6.0, ((0, 8), (1, 4)))
    gate_weight = centred(seeds[1], (D, TILE), D ** -0.5, 0.0625, ((1, 4),))
    up_weight = centred(seeds[2], (D, TILE), D ** -0.5, 0.0625, ((1, 4),))
    output_grad = centred(seeds[3], (TOKENS, TILES * TILE), (LENGTH ** -0.5), 0.15234375, ((0, 8), (1, 4)))
    input_basis = centred(seeds[4], (TILE, TILE), TILE ** -0.5, 0.1875, ((0, 8),), jnp.float32)
    output_basis = centred(seeds[5], (TILES, TILE, TILE), TILE ** -0.5, 0.1875, ((0, 4), (1, 8)), jnp.float32)
    shard_order = jax.random.permutation(seeds[6], SHARDS).astype(jnp.int32)
    return dict(tokens_in=tokens_in, gate_weight=gate_weight, up_weight=up_weight, output_grad=output_grad, input_basis=input_basis, output_basis=output_basis, shard_order=shard_order)


def reference(tokens_in, gate_weight, up_weight, output_grad, input_basis, output_basis, shard_order):
    gate_proj = jnp.dot(tokens_in, gate_weight, preferred_element_type=jnp.float32)
    up_proj = jnp.dot(tokens_in, up_weight, preferred_element_type=jnp.float32)
    hidden = (jax.nn.silu(gate_proj) * up_proj).astype(jnp.bfloat16)
    members = ((2 * shard_order) // SHARDS).astype(jnp.int32)
    token_member = jnp.repeat(members, TOK_DEV)
    gradients = []
    for sequence in range(2):
        chosen = (token_member == sequence).astype(jnp.bfloat16)
        masked = output_grad * chosen[:, None]
        gradients.append(jnp.dot(masked.T, hidden, preferred_element_type=jnp.float32))
    gradients = jnp.stack(gradients).reshape(2, TILES, TILE, TILE)
    halfway = jnp.einsum('skrc,cj->skrj', gradients, input_basis, precision=lax.Precision.HIGHEST)
    rotated = jnp.einsum('kri,skrj->skji', output_basis, halfway, precision=lax.Precision.HIGHEST)
    return jnp.mean(rotated * rotated, axis=0)
```

```python
import functools

import jax
import jax.numpy as jnp
from jax import lax
from jax.experimental import pallas as pl
from jax.experimental.pallas import tpu as pltpu
from jax.sharding import PartitionSpec as P

F32 = jnp.float32
BF16 = jnp.bfloat16
CHUNKS = 4


def split(value):
    high = value.astype(BF16)
    return high, (value - high.astype(F32)).astype(BF16)


def dot(a, b):
    return jnp.dot(a, b, preferred_element_type=F32)


def dot_first(a, b):
    return lax.dot_general(a, b, (((0,), (0,)), ((), ())), preferred_element_type=F32)


def kernel(
    n, order, tok_in, gate_in, up_in, grad_in, ib_in, ob_in, out,
    gate_w, up_w, tok, grad, ib, ob, acc_g, acc_u, hid,
    a_hi, a_lo, b_hi, b_lo, r_send, r_recv, sum0, sum1,
    load_sem, own_sem, x_send, x_recv, c_send, c_recv, f_send, f_recv,
    h_send, h_recv, ob_send, ob_recv, ib_send, ib_recv, e_send, e_recv,
    r_ssem, r_rsem,
):
    s, l = lax.axis_index("seq"), lax.axis_index("lane")
    px, pc = l // 2, l % 2
    part, across, diag = 2 * px + 1 - pc, 2 * (1 - px) + pc, 2 * (1 - px) + 1 - pc
    half = n // 2
    y, z = s % 2, s // 2
    ring = z + y * (n - 1 - 2 * z)

    def seq_of(r):
        r = lax.rem(r + 2 * n, n)
        b = r // half
        return (1 - b) * 2 * r + b * (2 * (n - 1 - r) + 1)

    nxt, prv = seq_of(ring + 1), seq_of(ring - 1)

    def remote(src, dst, ssem, rsem, seq, lane):
        return pltpu.make_async_remote_copy(
            src_ref=src, dst_ref=dst, send_sem=ssem, recv_sem=rsem,
            device_id=(seq, lane), device_id_type=pl.DeviceIdType.MESH,
        )

    loads = [
        pltpu.make_async_copy(gate_in, gate_w, load_sem.at[0]),
        pltpu.make_async_copy(up_in, up_w, load_sem.at[1]),
        pltpu.make_async_copy(grad_in, grad, load_sem.at[2]),
        pltpu.make_async_copy(ib_in, ib.at[s], load_sem.at[3]),
        pltpu.make_async_copy(ob_in, ob.at[s], load_sem.at[4]),
    ]
    depth = tok_in.shape[1]
    width = depth // CHUNKS
    own = [
        pltpu.make_async_copy(
            tok_in.at[:, pl.ds(i * width, width)], tok.at[0, i], own_sem.at[i]
        )
        for i in range(CHUNKS)
    ]
    for copy in loads + own:
        copy.start()

    barrier = pltpu.get_barrier_semaphore()
    for d in range(1, n):
        pl.semaphore_signal(
            barrier, inc=1, device_id=(lax.rem(s + d, n), l),
            device_id_type=pl.DeviceIdType.MESH,
        )
    for lane in (part, across):
        pl.semaphore_signal(
            barrier, inc=1, device_id=(s, lane), device_id_type=pl.DeviceIdType.MESH
        )
    pl.semaphore_wait(barrier, n + 1)

    to_across, to_part, passed = [], [], []
    for i in range(CHUNKS):
        piece = tok_in.at[:, pl.ds(i * width, width)]
        to_across.append(remote(piece, tok.at[2, i], x_send.at[i], x_recv.at[i], s, across))
        to_part.append(remote(piece, tok.at[1, i], c_send.at[i], c_recv.at[i], s, part))
        passed.append(remote(tok.at[2, i], tok.at[3, i], f_send.at[i], f_recv.at[i], s, part))
    for copy in to_across:
        copy.start()

    tile = ob.shape[2]
    wide = tile // 2
    narrow = tile // 4
    ib_base = pc * wide

    def ring_copies(t):
        made = []
        for way in range(2):
            owner = seq_of(ring - t) if way == 0 else seq_of(ring + t)
            target = nxt if way == 0 else prv
            columns = pl.ds(way * wide, wide)
            small = pl.ds(pl.multiple_of(ib_base + way * narrow, narrow), narrow)
            ob_src = ob_in.at[:, columns] if t == 0 else ob.at[owner, :, columns]
            ib_src = ib_in.at[:, small] if t == 0 else ib.at[owner, :, small]
            made.append(remote(
                ob_src, ob.at[owner, :, columns],
                ob_send.at[way, t], ob_recv.at[way, t], target, l))
            made.append(remote(
                ib_src, ib.at[owner, :, small],
                ib_send.at[way, t], ib_recv.at[way, t], target, l))
        return made

    steps = [ring_copies(t) for t in range(n - 1)]
    swaps = []

    def ring_arrive(t):
        for copy in steps[t]:
            copy.wait_recv()
        if t + 1 < n - 1:
            for copy in steps[t + 1]:
                copy.start()
        for way in range(2):
            owner = seq_of(ring - t - 1) if way == 0 else seq_of(ring + t + 1)
            small = pl.ds(pl.multiple_of(ib_base + way * narrow, narrow), narrow)
            piece = ib.at[owner, :, small]
            swap = remote(piece, piece, e_send.at[way, t], e_recv.at[way, t], s, part)
            swap.start()
            swaps.append(swap)

    for copy in steps[0]:
        copy.start()
    for copy in to_part:
        copy.start()

    loads[0].wait()
    loads[1].wait()

    def multiply(slot, i, lane, first=False):
        rows = pl.ds(pl.multiple_of(lane * depth + i * width, width), width)
        piece = tok[slot, i]
        g = dot(piece, gate_w[rows, :])
        u = dot(piece, up_w[rows, :])
        if first:
            acc_g[...] = g
            acc_u[...] = u
        else:
            acc_g[...] += g
            acc_u[...] += u

    def arrive(i):
        to_across[i].wait_recv()
        passed[i].start()
        multiply(2, i, across)
        passed[i].wait_recv()
        multiply(3, i, diag)

    for i in range(CHUNKS):
        own[i].wait()
        multiply(0, i, l, first=i == 0)
    for i in range(CHUNKS):
        to_part[i].wait_recv()
        multiply(1, i, part)

    done = 0
    for i in range(CHUNKS):
        upto = min(n - 1, ((i + 1) * 5 * (n - 1)) // (7 * CHUNKS))
        while done < upto:
            ring_arrive(done)
            done += 1
        arrive(i)

    gate = acc_g[...]
    hid[0] = (gate / (1.0 + jnp.exp(-gate)) * acc_u[...]).astype(BF16)
    h_across = remote(hid.at[0], hid.at[2], h_send.at[0], h_recv.at[0], s, across)
    h_part = remote(hid.at[0], hid.at[1], h_send.at[1], h_recv.at[1], s, part)
    h_pass = remote(hid.at[2], hid.at[3], h_send.at[2], h_recv.at[2], s, part)
    h_across.start()
    h_part.start()
    while done < n - 1:
        ring_arrive(done)
        done += 1
    loads[3].wait()
    loads[4].wait()
    loads[2].wait()
    h_across.wait_recv()
    h_pass.start()

    a = dot(grad[...], ob[...].reshape(tile, tile))
    high, low = split(a)
    a_hi[...] = high
    a_lo[...] = low

    h_part.wait_recv()
    for swap in swaps:
        swap.wait_recv()
    h_pass.wait_recv()
    units = hid.shape[2]
    rows_dev = ib.shape[1]
    count = units // rows_dev
    pieces = []
    for slot, lane in ((0, l), (1, part), (2, across), (3, diag)):
        block = ib[pl.ds(lane * count, count)].reshape(units, tile)
        i_hi, i_lo = split(block)
        h = hid[slot]
        pieces.append(dot(h, i_hi) + dot(h, i_lo))
    high, low = split((pieces[0] + pieces[1]) + (pieces[2] + pieces[3]))
    b_hi[...] = high
    b_lo[...] = low

    group = max(1, 128 // rows_dev)
    size = group * rows_dev
    blocks = n // group

    def sends(dest):
        return remote(
            r_send.at[dest], r_recv.at[s], r_ssem.at[dest], r_rsem.at[s], dest, l)

    def emit(q):
        columns = pl.ds(pl.multiple_of(q * size, size), size)
        bh, bl = b_hi[:, columns], b_lo[:, columns]
        ah, al = a_hi[...], a_lo[...]
        r = dot_first(bh, ah) + (dot_first(bh, al) + dot_first(bl, ah))
        r_send[pl.ds(q * group, group)] = r.astype(BF16).reshape(group, rows_dev, tile)

    @pl.loop(0, blocks)
    def _(d):
        q = lax.rem(s // group + 1 + d, blocks)
        emit(q)
        for g in range(group):
            dest = q * group + g

            @pl.when(dest != s)
            def _():
                sends(dest).start()

    def masks(src):
        member = (2 * order[src]) // n
        second = member.astype(F32)
        return 1.0 - second, second

    first, second = masks(s)
    mine = r_send[s].astype(F32)
    sum0[...] = mine * first
    sum1[...] = mine * second

    @pl.loop(1, n)
    def _(d):
        src = lax.rem(s + n - d, n)
        remote(
            r_send.at[src], r_recv.at[src], r_ssem.at[src], r_rsem.at[src], src, l
        ).wait_recv()
        first, second = masks(src)
        value = r_recv[src].astype(F32)
        sum0[...] += value * first
        sum1[...] += value * second

    r0, r1 = sum0[...], sum1[...]
    out[0] = (r0 * r0 + r1 * r1) * 0.5

    @pl.loop(1, n)
    def _(d):
        sends(lax.rem(s + d, n)).wait_send()

    for copy in to_across + to_part + passed + [h_across, h_part, h_pass] + swaps:
        copy.wait_send()
    for made in steps:
        for copy in made:
            copy.wait_send()


def on_device(
    tokens_in, gate_weight, up_weight, output_grad, input_basis, output_basis, shard_order
):
    n = lax.axis_size("seq")
    tokens, depth = tokens_in.shape
    units = gate_weight.shape[1]
    rows, tile = input_basis.shape
    sem = pltpu.SemaphoreType.DMA
    any_spec = pl.BlockSpec(memory_space=pl.ANY)
    return pl.pallas_call(
        functools.partial(kernel, n),
        out_shape=jax.ShapeDtypeStruct((1, rows, tile), F32),
        in_specs=[pl.BlockSpec(memory_space=pltpu.SMEM)] + [any_spec] * 6,
        out_specs=pl.BlockSpec(memory_space=pltpu.VMEM),
        scratch_shapes=[
            pltpu.VMEM(gate_weight.shape, BF16),
            pltpu.VMEM(up_weight.shape, BF16),
            pltpu.VMEM((4, CHUNKS, tokens, depth // CHUNKS), BF16),
            pltpu.VMEM((tokens, tile), BF16),
            pltpu.VMEM((n, rows, tile), F32),
            pltpu.VMEM((n, rows, tile), BF16),
            pltpu.VMEM((tokens, units), F32),
            pltpu.VMEM((tokens, units), F32),
            pltpu.VMEM((4, tokens, units), BF16),
            pltpu.VMEM((tokens, tile), BF16),
            pltpu.VMEM((tokens, tile), BF16),
            pltpu.VMEM((tokens, tile), BF16),
            pltpu.VMEM((tokens, tile), BF16),
            pltpu.VMEM((n, rows, tile), BF16),
            pltpu.VMEM((n, rows, tile), BF16),
            pltpu.VMEM((rows, tile), F32),
            pltpu.VMEM((rows, tile), F32),
            sem((5,)), sem((CHUNKS,)),
            sem((CHUNKS,)), sem((CHUNKS,)), sem((CHUNKS,)), sem((CHUNKS,)),
            sem((CHUNKS,)), sem((CHUNKS,)),
            sem((3,)), sem((3,)),
            sem((2, n - 1)), sem((2, n - 1)), sem((2, n - 1)), sem((2, n - 1)),
            sem((2, n - 1)), sem((2, n - 1)),
            sem((n,)), sem((n,)),
        ],
        compiler_params=pltpu.CompilerParams(
            collective_id=0, has_side_effects=True, vmem_limit_bytes=60 * 2**20
        ),
    )(
        shard_order, tokens_in, gate_weight, up_weight, output_grad,
        input_basis, output_basis[0].astype(BF16),
    )


def solution(mesh):
    return jax.shard_map(
        on_device,
        mesh=mesh,
        in_specs=(
            P("seq", "lane"),
            P(None, "lane"),
            P(None, "lane"),
            P("seq", "lane"),
            P("seq", None),
            P("lane", "seq", None),
            P(),
        ),
        out_specs=P("lane", "seq", None),
        check_vma=False,
    )
```

```python
import functools

import jax
import jax.numpy as jnp
from jax import lax
from jax.experimental import pallas as pl
from jax.experimental.pallas import tpu as pltpu
from jax.sharding import PartitionSpec as P

F32 = jnp.float32
BF16 = jnp.bfloat16
CHUNKS = 4


def split(value):
    high = value.astype(BF16)
    return high, (value - high.astype(F32)).astype(BF16)


def dot(a, b):
    return jnp.dot(a, b, preferred_element_type=F32)


def dot_first(a, b):
    return lax.dot_general(a, b, (((0,), (0,)), ((), ())), preferred_element_type=F32)


def kernel(
    n, order, tok_in, gate_in, up_in, grad_in, ib_in, ob_in, out,
    gate_w, up_w, tok, grad, ib, ob, acc_g, acc_u, hid,
    a_hi, a_lo, b_hi, b_lo, r_send, r_recv, sum0, sum1,
    load_sem, own_sem, x_send, x_recv, c_send, c_recv, f_send, f_recv,
    h_send, h_recv, ob_send, ob_recv, ib_send, ib_recv, e_send, e_recv,
    r_ssem, r_rsem,
):
    s, l = lax.axis_index("seq"), lax.axis_index("lane")
    px, pc = l // 2, l % 2
    part, across, diag = 2 * px + 1 - pc, 2 * (1 - px) + pc, 2 * (1 - px) + 1 - pc
    half = n // 2
    y, z = s % 2, s // 2
    ring = z + y * (n - 1 - 2 * z)

    def seq_of(r):
        r = lax.rem(r + 2 * n, n)
        b = r // half
        return (1 - b) * 2 * r + b * (2 * (n - 1 - r) + 1)

    nxt, prv = seq_of(ring + 1), seq_of(ring - 1)

    def remote(src, dst, ssem, rsem, seq, lane):
        return pltpu.make_async_remote_copy(
            src_ref=src, dst_ref=dst, send_sem=ssem, recv_sem=rsem,
            device_id=(seq, lane), device_id_type=pl.DeviceIdType.MESH,
        )

    loads = [
        pltpu.make_async_copy(gate_in, gate_w, load_sem.at[0]),
        pltpu.make_async_copy(up_in, up_w, load_sem.at[1]),
        pltpu.make_async_copy(grad_in, grad, load_sem.at[2]),
        pltpu.make_async_copy(ib_in, ib.at[s], load_sem.at[3]),
        pltpu.make_async_copy(ob_in, ob.at[s], load_sem.at[4]),
    ]
    depth = tok_in.shape[1]
    width = depth // CHUNKS
    own = [
        pltpu.make_async_copy(
            tok_in.at[:, pl.ds(i * width, width)], tok.at[0, i], own_sem.at[i]
        )
        for i in range(CHUNKS)
    ]
    for copy in loads + own:
        copy.start()

    barrier = pltpu.get_barrier_semaphore()
    for d in range(1, n):
        pl.semaphore_signal(
            barrier, inc=1, device_id=(lax.rem(s + d, n), l),
            device_id_type=pl.DeviceIdType.MESH,
        )
    for lane in (part, across):
        pl.semaphore_signal(
            barrier, inc=1, device_id=(s, lane), device_id_type=pl.DeviceIdType.MESH
        )
    pl.semaphore_wait(barrier, n + 1)

    to_across, to_part, passed = [], [], []
    for i in range(CHUNKS):
        piece = tok_in.at[:, pl.ds(i * width, width)]
        to_across.append(remote(piece, tok.at[2, i], x_send.at[i], x_recv.at[i], s, across))
        to_part.append(remote(piece, tok.at[1, i], c_send.at[i], c_recv.at[i], s, part))
        passed.append(remote(tok.at[2, i], tok.at[3, i], f_send.at[i], f_recv.at[i], s, part))
    for copy in to_across:
        copy.start()

    tile = ob.shape[2]
    wide = tile // 2
    narrow = tile // 4
    ib_base = pc * wide

    def ring_copies(t):
        made = []
        for way in range(2):
            owner = seq_of(ring - t) if way == 0 else seq_of(ring + t)
            target = nxt if way == 0 else prv
            columns = pl.ds(way * wide, wide)
            small = pl.ds(pl.multiple_of(ib_base + way * narrow, narrow), narrow)
            ob_src = ob_in.at[:, columns] if t == 0 else ob.at[owner, :, columns]
            ib_src = ib_in.at[:, small] if t == 0 else ib.at[owner, :, small]
            made.append(remote(
                ob_src, ob.at[owner, :, columns],
                ob_send.at[way, t], ob_recv.at[way, t], target, l))
            made.append(remote(
                ib_src, ib.at[owner, :, small],
                ib_send.at[way, t], ib_recv.at[way, t], target, l))
        return made

    steps = [ring_copies(t) for t in range(n - 1)]
    swaps = []

    def ring_arrive(t):
        for j, copy in enumerate(steps[t]):
            copy.wait_recv()
            if t + 1 < n - 1:
                steps[t + 1][j].start()
        for way in range(2):
            owner = seq_of(ring - t - 1) if way == 0 else seq_of(ring + t + 1)
            small = pl.ds(pl.multiple_of(ib_base + way * narrow, narrow), narrow)
            piece = ib.at[owner, :, small]
            swap = remote(piece, piece, e_send.at[way, t], e_recv.at[way, t], s, part)
            swap.start()
            swaps.append(swap)

    for copy in steps[0]:
        copy.start()
    for copy in to_part:
        copy.start()

    loads[0].wait()
    loads[1].wait()

    def multiply(slot, i, lane, first=False):
        rows = pl.ds(pl.multiple_of(lane * depth + i * width, width), width)
        piece = tok[slot, i]
        g = dot(piece, gate_w[rows, :])
        u = dot(piece, up_w[rows, :])
        if first:
            acc_g[...] = g
            acc_u[...] = u
        else:
            acc_g[...] += g
            acc_u[...] += u

    def arrive(i):
        to_across[i].wait_recv()
        passed[i].start()
        multiply(2, i, across)
        passed[i].wait_recv()
        multiply(3, i, diag)

    for i in range(CHUNKS):
        own[i].wait()
        multiply(0, i, l, first=i == 0)
    for i in range(CHUNKS):
        to_part[i].wait_recv()
        multiply(1, i, part)

    done = 0
    for i in range(CHUNKS):
        upto = 5 * (n - 1) // 7
        while done < upto:
            ring_arrive(done)
            done += 1
        arrive(i)

    gate = acc_g[...]
    hid[0] = (gate / (1.0 + jnp.exp(-gate)) * acc_u[...]).astype(BF16)
    h_across = remote(hid.at[0], hid.at[2], h_send.at[0], h_recv.at[0], s, across)
    h_part = remote(hid.at[0], hid.at[1], h_send.at[1], h_recv.at[1], s, part)
    h_pass = remote(hid.at[2], hid.at[3], h_send.at[2], h_recv.at[2], s, part)
    h_across.start()
    h_part.start()
    while done < n - 1:
        ring_arrive(done)
        done += 1
    loads[3].wait()
    loads[4].wait()
    loads[2].wait()
    a = dot(grad[...], ob[...].reshape(tile, tile))
    high, low = split(a)
    a_hi[...] = high
    a_lo[...] = low
    h_across.wait_recv()
    h_pass.start()

    h_part.wait_recv()
    for swap in swaps:
        swap.wait_recv()
    h_pass.wait_recv()
    units = hid.shape[2]
    rows_dev = ib.shape[1]
    count = units // rows_dev
    pieces = []
    for slot, lane in ((0, l), (1, part), (2, across), (3, diag)):
        block = ib[pl.ds(lane * count, count)].reshape(units, tile)
        i_hi, i_lo = split(block)
        h = hid[slot]
        pieces.append(dot(h, i_hi) + dot(h, i_lo))
    high, low = split((pieces[0] + pieces[1]) + (pieces[2] + pieces[3]))
    b_hi[...] = high
    b_lo[...] = low

    group = max(1, 128 // rows_dev)
    size = group * rows_dev
    blocks = n // group

    def sends(dest):
        return remote(
            r_send.at[dest], r_recv.at[s], r_ssem.at[dest], r_rsem.at[s], dest, l)

    def emit(q):
        columns = pl.ds(pl.multiple_of(q * size, size), size)
        bh, bl = b_hi[:, columns], b_lo[:, columns]
        ah, al = a_hi[...], a_lo[...]
        r = dot_first(bh, ah) + (dot_first(bh, al) + dot_first(bl, ah))
        r_send[pl.ds(q * group, group)] = r.astype(BF16).reshape(group, rows_dev, tile)

    @pl.loop(0, blocks)
    def _(d):
        q = lax.rem(s // group + 1 + d, blocks)
        emit(q)
        for g in range(group):
            dest = q * group + g

            @pl.when(dest != s)
            def _():
                sends(dest).start()

    def masks(src):
        member = (2 * order[src]) // n
        second = member.astype(F32)
        return 1.0 - second, second

    first, second = masks(s)
    mine = r_send[s].astype(F32)
    sum0[...] = mine * first
    sum1[...] = mine * second

    @pl.loop(1, n)
    def _(d):
        src = lax.rem(s + n - d, n)
        remote(
            r_send.at[src], r_recv.at[src], r_ssem.at[src], r_rsem.at[src], src, l
        ).wait_recv()
        first, second = masks(src)
        value = r_recv[src].astype(F32)
        sum0[...] += value * first
        sum1[...] += value * second

    r0, r1 = sum0[...], sum1[...]
    out[0] = (r0 * r0 + r1 * r1) * 0.5

    @pl.loop(1, n)
    def _(d):
        sends(lax.rem(s + d, n)).wait_send()

    for copy in to_across + to_part + passed + [h_across, h_part, h_pass] + swaps:
        copy.wait_send()
    for made in steps:
        for copy in made:
            copy.wait_send()


def on_device(
    tokens_in, gate_weight, up_weight, output_grad, input_basis, output_basis, shard_order
):
    n = lax.axis_size("seq")
    tokens, depth = tokens_in.shape
    units = gate_weight.shape[1]
    rows, tile = input_basis.shape
    sem = pltpu.SemaphoreType.DMA
    any_spec = pl.BlockSpec(memory_space=pl.ANY)
    return pl.pallas_call(
        functools.partial(kernel, n),
        out_shape=jax.ShapeDtypeStruct((1, rows, tile), F32),
        in_specs=[pl.BlockSpec(memory_space=pltpu.SMEM)] + [any_spec] * 6,
        out_specs=pl.BlockSpec(memory_space=pltpu.VMEM),
        scratch_shapes=[
            pltpu.VMEM(gate_weight.shape, BF16),
            pltpu.VMEM(up_weight.shape, BF16),
            pltpu.VMEM((4, CHUNKS, tokens, depth // CHUNKS), BF16),
            pltpu.VMEM((tokens, tile), BF16),
            pltpu.VMEM((n, rows, tile), F32),
            pltpu.VMEM((n, rows, tile), BF16),
            pltpu.VMEM((tokens, units), F32),
            pltpu.VMEM((tokens, units), F32),
            pltpu.VMEM((4, tokens, units), BF16),
            pltpu.VMEM((tokens, tile), BF16),
            pltpu.VMEM((tokens, tile), BF16),
            pltpu.VMEM((tokens, tile), BF16),
            pltpu.VMEM((tokens, tile), BF16),
            pltpu.VMEM((n, rows, tile), BF16),
            pltpu.VMEM((n, rows, tile), BF16),
            pltpu.VMEM((rows, tile), F32),
            pltpu.VMEM((rows, tile), F32),
            sem((5,)), sem((CHUNKS,)),
            sem((CHUNKS,)), sem((CHUNKS,)), sem((CHUNKS,)), sem((CHUNKS,)),
            sem((CHUNKS,)), sem((CHUNKS,)),
            sem((3,)), sem((3,)),
            sem((2, n - 1)), sem((2, n - 1)), sem((2, n - 1)), sem((2, n - 1)),
            sem((2, n - 1)), sem((2, n - 1)),
            sem((n,)), sem((n,)),
        ],
        compiler_params=pltpu.CompilerParams(
            collective_id=0, has_side_effects=True, vmem_limit_bytes=60 * 2**20
        ),
    )(
        shard_order, tokens_in, gate_weight, up_weight, output_grad,
        input_basis, output_basis[0].astype(BF16),
    )


def solution(mesh):
    return jax.shard_map(
        on_device,
        mesh=mesh,
        in_specs=(
            P("seq", "lane"),
            P(None, "lane"),
            P(None, "lane"),
            P("seq", "lane"),
            P("seq", None),
            P("lane", "seq", None),
            P(),
        ),
        out_specs=P("lane", "seq", None),
        check_vma=False,
    )
```
